128 devices in a mesh: ctx: 32 (over z, y, x_lo), head: 4 (over x_hi, core).
Axes of the slice: x: 4 (x_hi: 2, x_lo: 2; x = x_hi * 2 + x_lo), y: 4, z: 4, core: 2. Of those that a mesh axis runs over, the one named last changes fastest.
Arguments:
- tokens: bfloat16 [12288, 4096], P('ctx', 'head'), may hold values from -6 to 6
- doc_ids: int32 [12288], replicated, may hold values from 0 to 3, never falling along the last dimension, each value on 1 to 9216 neighbouring positions
- norm_gain: float32 [4096], replicated, may hold values from 0.25 to 1.75
- w_query: bfloat16 [4096, 4096], P(None, 'head'), may hold values from -4 to 4
- w_key: bfloat16 [4096, 1024], P(None, 'head'), may hold values from -0.09375 to 0.09375
- w_value: bfloat16 [4096, 1024], P(None, 'head'), may hold values from -0.09375 to 0.09375
- w_out: bfloat16 [4096, 4096], P('head'), may hold values from -0.09375 to 0.09375
Outputs:
- layer_out: bfloat16 [12288, 4096], P('ctx', 'head')
The draws below stay inside these ranges and needn't reach their ends.
Inputs may be any that keep to these rules, and one draw needn't show every extreme that they name: `doc_ids`: never falling along the sequence; 4 documents, one of exactly 9216 tokens.
All inputs are finite; a program needn't handle non-finite values.
Results may differ from the reference program's by a relative error of at most 0.012.
The reference program's roundings to bfloat16 on the way count: a program that leaves them out, or rounds other values in their place, can miss the bound.
Values may be sent and summed in bfloat16 or wider, within the bound.
A program may use at most 128 MiB of HBM per device.

```python
import math
import jax
import jax.numpy as jnp
import numpy as np
from jax import lax

D = 4096
HQ = 32
KVH = 8
HD = 128
TOK_DEV = 384
DOCS = 4
TOKENS = 12288
N_CTX = 32


def draw_w_query(key, part):
    sample = jax.random.truncated_normal(key, -6.0, 6.0, (D, HQ * HD), jnp.float32) * D ** (-0.5)
    sample = jnp.clip(sample, -4.0, 4.0)
    return sample.astype(jnp.bfloat16)


def shard_levels(own_key, dims, split, least, largest):
    loudness = 1.0
    for axis_at, blocks in split:
        heights = jax.random.uniform(jax.random.fold_in(jax.random.fold_in(own_key, 6), axis_at), (blocks,), jnp.float32, least / len(split), largest / len(split))
        loudness = loudness * jnp.repeat(jnp.exp(heights), dims[axis_at] // blocks).reshape((-1,) + (1,) * (len(dims) - 1 - axis_at))
    return loudness


def split_up(amount, total, limit, lean):
    portions = [(1 << 20) // math.isqrt(grade ** lean) + 1 for grade in range(2, amount + 1)]
    surplus, holding = total - limit - (amount - 1), [1] * (amount - 1)
    while surplus > 0:
        candidates = [i for i in range(amount - 1) if holding[i] < limit]
        pool, left = sum([portions[i] for i in candidates]), surplus
        for i in candidates:
            more = min(limit - holding[i], max(1, left * portions[i] // pool), surplus)
            holding[i] = holding[i] + more
            surplus = surplus - more
    return np.array([limit] + holding)


def ragged_sizes(key, number_of, total, reach, lean):
    if number_of == 2:
        one = jax.random.randint(key, (), max(1, total - reach), min(reach, total - 1) + 1)
        return jnp.stack([one, total - one])
    sizes = jnp.asarray(split_up(number_of, total, reach, lean), jnp.int32)
    twos = (number_of - 1) // 2
    donor, sink = sizes[1:1 + 2 * twos:2], sizes[2:2 + 2 * twos:2]
    margin = jnp.minimum(donor - 1, reach - sink)
    moved = jax.random.randint(jax.random.fold_in(key, 1), (twos,), 0, 1 << 20) % (margin + 1)
    sizes = sizes.at[1:1 + 2 * twos:2].set(donor - moved).at[2:2 + 2 * twos:2].set(sink + moved)
    return sizes[jax.random.permutation(jax.random.fold_in(key, 2), number_of)]


def gaussian(stream_key, extent, scale, reach, pieces=(), kind=jnp.bfloat16):
    level = shard_levels(stream_key, extent, pieces, -0.22, 0.18) if pieces else 1.0
    array = jax.random.normal(stream_key, extent, jnp.float32) * scale * level
    return jnp.minimum(jnp.maximum(array, -reach), reach).astype(kind)


def setup_inputs(seed: int = 0) -> dict:
    arg_keys = jax.random.split(jax.random.key(seed), 8)
    tokens = gaussian(arg_keys[0], (TOKENS, D), 1.0, 6.0, ((0, 32), (1, 4)))
    doc_ids = jnp.searchsorted(jnp.cumsum(ragged_sizes(arg_keys[1], DOCS, TOKENS, 3 * TOKENS // 4, 2)), jnp.arange(TOKENS), side="right").astype(jnp.int32)
    norm_gain = jnp.clip(1.0 + 0.15 * jax.random.normal(arg_keys[2], (D,), jnp.float32), 0.25, 1.75)
    w_query = draw_w_query(jax.random.fold_in(arg_keys[7], 71), 0)
    w_key = gaussian(arg_keys[4], (D, KVH * HD), D ** -0.5, 0.09375, ((1, 4),))
    w_value = gaussian(arg_keys[5], (D, KVH * HD), D ** -0.5, 0.09375, ((1, 4),))
    w_out = gaussian(arg_keys[6], (HQ * HD, D), (HQ * HD) ** -0.5, 0.09375, ((0, 4),))
    return dict(tokens=tokens, doc_ids=doc_ids, norm_gain=norm_gain, w_query=w_query, w_key=w_key, w_value=w_value, w_out=w_out)


THETA = 500000.0

def rotate(values, positions):
    head_width = values.shape[-1]
    midpoint = head_width // 2
    exponents = jnp.arange(midpoint, dtype=jnp.float32) * (2.0 / head_width)
    inverse = jnp.power(jnp.float32(THETA), -exponents)
    angles = positions.astype(jnp.float32)[:, None] * inverse[None, :]
    cosine = jnp.cos(angles)[:, None, :]
    sine_wave = jnp.sin(angles)[:, None, :]
    lower_half = values[..., :midpoint]
    upper_half = values[..., midpoint:]
    return jnp.concatenate([lower_half * cosine - upper_half * sine_wave, upper_half * cosine + lower_half * sine_wave], axis=-1)

def reference(tokens, doc_ids, norm_gain, w_query, w_key, w_value, w_out):
    floats = tokens.astype(jnp.float32)
    spread = lax.optimization_barrier(jnp.mean(floats * floats, axis=-1, keepdims=True))
    normed = (floats * lax.rsqrt(spread + 1e-05) * norm_gain[None, :]).astype(jnp.bfloat16)
    positions = jnp.arange(TOKENS, dtype=jnp.int32)
    queries = jnp.dot(normed, w_query, preferred_element_type=jnp.float32).reshape(TOKENS, HQ, HD)
    queries = rotate(queries, positions).astype(jnp.bfloat16)
    keys_all = jnp.dot(normed, w_key, preferred_element_type=jnp.float32).reshape(TOKENS, KVH, HD)
    keys_all = rotate(keys_all, positions).astype(jnp.bfloat16)
    values_all = jnp.dot(normed, w_value, preferred_element_type=jnp.float32).astype(jnp.bfloat16).reshape(TOKENS, KVH, HD)
    starts = jnp.searchsorted(doc_ids, doc_ids, side='left').astype(jnp.int32)
    query_heads = jnp.transpose(queries, (1, 0, 2))
    key_heads = jnp.transpose(keys_all, (1, 0, 2))
    value_heads = jnp.transpose(values_all, (1, 0, 2))
    group_size = HQ // KVH
    score_scale = HD ** (-0.5)

    def one_head(head_index):
        query_rows = query_heads[head_index]
        key_rows = key_heads[head_index // group_size]
        value_rows = value_heads[head_index // group_size]

        def one_block(block_index):
            row_start = block_index * TOK_DEV
            block_queries = lax.dynamic_slice_in_dim(query_rows, row_start, TOK_DEV, 0)
            block_positions = lax.dynamic_slice_in_dim(positions, row_start, TOK_DEV, 0)
            block_starts = lax.dynamic_slice_in_dim(starts, row_start, TOK_DEV, 0)
            scores = jnp.dot(block_queries, key_rows.T, preferred_element_type=jnp.float32) * score_scale
            allowed = (positions[None, :] <= block_positions[:, None]) & (positions[None, :] >= block_starts[:, None])
            scores = jnp.where(allowed, scores, -jnp.inf)
            highest = lax.optimization_barrier(jnp.max(scores, axis=-1, keepdims=True))
            weights = jnp.where(allowed, jnp.exp(scores - highest), 0.0)
            denominator = lax.optimization_barrier(jnp.sum(weights, axis=-1, keepdims=True))
            combined = jnp.dot(weights.astype(jnp.bfloat16), value_rows, preferred_element_type=jnp.float32)
            return combined / denominator
        return lax.map(one_block, jnp.arange(N_CTX, dtype=jnp.int32)).reshape(TOKENS, HD)
    heads_out = lax.map(one_head, jnp.arange(HQ, dtype=jnp.int32))
    attended = jnp.transpose(heads_out, (1, 0, 2)).reshape(TOKENS, HQ * HD).astype(jnp.bfloat16)
    return (floats + jnp.dot(attended, w_out, preferred_element_type=jnp.float32)).astype(jnp.bfloat16)
```

```python
import functools
import math

import jax
import jax.numpy as jnp
import numpy as np
from jax import lax
from jax.experimental import pallas as pl
from jax.experimental.pallas import tpu as pltpu
from jax.sharding import PartitionSpec as P

MESH = pl.DeviceIdType.MESH
BF16 = jnp.bfloat16
F32 = jnp.float32
HD = 128
GROUP = 4
THETA = 500000.0
QR = 96
KB = 1024
VMEM_LIMIT = 60 * 2**20


def position():
    c, h = lax.axis_index("ctx"), lax.axis_index("head")
    return lax.div(h, 2), lax.rem(c, 2), lax.rem(lax.div(c, 2), 4), lax.div(c, 8), lax.rem(h, 2)


def device(xhi, xlo, y, z, core):
    return {"ctx": (z * 4 + y) * 2 + xlo, "head": xhi * 2 + core}


def wrap(v):
    return lax.rem(v + 4, 4)


def greet(peers):
    barrier = pltpu.get_barrier_semaphore()
    for peer in peers:
        pl.semaphore_signal(barrier, inc=1, device_id=peer, device_id_type=MESH)
    pl.semaphore_wait(barrier, len(peers))


def remote(src, dst, send, recv, peer):
    return pltpu.make_async_remote_copy(
        src_ref=src, dst_ref=dst, send_sem=send, recv_sem=recv, device_id=peer, device_id_type=MESH
    )


def rope_tables(rows, blocks):
    inverse = THETA ** (-np.arange(HD // 2, dtype=np.float64) / (HD // 2))
    near = np.arange(rows, dtype=np.float64)[:, None] * inverse[None, :]
    far = (np.arange(blocks, dtype=np.float64) * rows)[:, None] * inverse[None, :]

    def pair(a):
        return (
            np.concatenate([np.cos(a), np.cos(a)], 1).astype(np.float32),
            np.concatenate([np.sin(a), np.sin(a)], 1).astype(np.float32),
        )

    return pair(near) + pair(far)


def project_kernel(
    x_ref, gain_ref, cn_ref, sn_ref, cf_ref, sf_ref, wq_hbm, wk_hbm, wv_hbm,
    q_ref, kv_ref,
    xbuf, nbuf, wq, wk, wv, wsem, lsem, ssend, srecv, osend, orecv, fsend, frecv,
):
    xhi, xlo, y, z, core = position()
    head = xhi * 2 + core
    rows = x_ref.shape[0]
    nch = xbuf.shape[0]
    ch = rows // nch
    sib, opp = device(xhi, xlo, y, z, 1 - core), device(1 - xhi, xlo, y, z, core)
    hs, ho, hf = xhi * 2 + 1 - core, (1 - xhi) * 2 + core, (1 - xhi) * 2 + 1 - core
    loads = [
        pltpu.make_async_copy(a, b, wsem.at[i])
        for i, (a, b) in enumerate(((wk_hbm, wk), (wv_hbm, wv), (wq_hbm, wq)))
    ]
    greet([sib, opp])
    outs, sibs, owns = [], [], []
    for k in range(nch):
        src = x_ref.at[pl.ds(k * ch, ch)]
        outs.append(remote(src, xbuf.at[k, head], osend.at[k], orecv.at[k], opp))
        sibs.append(remote(src, xbuf.at[k, head], ssend.at[k], srecv.at[k], sib))
        owns.append(pltpu.make_async_copy(src, xbuf.at[k, head], lsem.at[k]))
        outs[k].start()
    for k in range(nch):
        sibs[k].start()
        owns[k].start()
    for load in loads:
        load.start()
    cn, sn = cn_ref[...], sn_ref[...]
    ctx = lax.axis_index("ctx")
    cf, sf = cf_ref[pl.ds(ctx, 1), :], sf_ref[pl.ds(ctx, 1), :]
    cos = cn * cf - sn * sf
    sin = sn * cf + cn * sf
    lane = lax.broadcasted_iota(jnp.int32, (rows, HD), 1)
    sin = jnp.where(lane < HD // 2, -sin, sin)

    def rope(v, k):
        lo = k * ch
        return v * cos[lo:lo + ch] + pltpu.roll(v, HD // 2, 1) * sin[lo:lo + ch]

    forwards = []
    for k in range(nch):
        remote(x_ref.at[pl.ds(k * ch, ch)], xbuf.at[k, ho], osend.at[k], orecv.at[k], opp).wait_recv()
        f = remote(xbuf.at[k, ho], xbuf.at[k, ho], fsend.at[k], frecv.at[k], sib)
        f.start()
        forwards.append(f)
        owns[k].wait()
        remote(x_ref.at[pl.ds(k * ch, ch)], xbuf.at[k, hs], ssend.at[k], srecv.at[k], sib).wait_recv()
        remote(xbuf.at[k, ho], xbuf.at[k, hf], fsend.at[k], frecv.at[k], sib).wait_recv()
        total = jnp.zeros((ch, 1), F32)
        width = x_ref.shape[1]
        for j in range(4):
            v = xbuf[k, j].astype(F32)
            total = total + jnp.sum(v * v, axis=1, keepdims=True)
        scale = lax.rsqrt(total / (4.0 * width) + 1e-05)
        for j in range(4):
            v = xbuf[k, j].astype(F32)
            nbuf[:, j * width:(j + 1) * width] = (
                v * scale * gain_ref[:, j * width:(j + 1) * width]
            ).astype(BF16)
        if k == 0:
            loads[0].wait()
            loads[1].wait()
        kk = jnp.dot(nbuf[...], wk[...], preferred_element_type=F32)
        vv = jnp.dot(nbuf[...], wv[...], preferred_element_type=F32)
        for hh in range(2):
            kv_ref[0, hh, k * ch:(k + 1) * ch, :] = rope(kk[:, hh * HD:(hh + 1) * HD], k).astype(BF16)
            kv_ref[1, hh, k * ch:(k + 1) * ch, :] = vv[:, hh * HD:(hh + 1) * HD].astype(BF16)
        if k == 0:
            loads[2].wait()
        for pairs in range(4):
            qq = jnp.dot(
                nbuf[...], wq[:, pairs * 256:(pairs + 1) * 256], preferred_element_type=F32
            )
            for u in range(2):
                g = (pairs % 2) * 2 + u
                out = rope(qq[:, u * HD:(u + 1) * HD], k).astype(BF16)
                for b in range(ch // QR):
                    gb = k * (ch // QR) + b
                    at = (gb // 2) * GROUP * QR + g * QR
                    q_ref[pairs // 2, gb % 2, at:at + QR, :] = out[b * QR:(b + 1) * QR]
    for k in range(nch):
        outs[k].wait_send()
        sibs[k].wait_send()
        forwards[k].wait_send()


def exchange_kernel(
    q_ref, kv_ref, qo_ref, kvo_ref,
    zsend, zrecv, qsend, qrecv, xsend, xrecv, ypsend, yprecv, ymsend, ymrecv, fsend, frecv, bsend, brecv,
):
    xhi, xlo, y, z, core = position()
    rows = kv_ref.shape[2]
    sib = device(xhi, xlo, y, z, 1 - core)
    side = device(xhi, 1 - xlo, y, z, core)
    up, down = device(xhi, xlo, wrap(y + 1), z, core), device(xhi, xlo, wrap(y - 1), z, core)
    ring = [device(xhi, xlo, y, wrap(z + d), c) for d in (1, 2, 3) for c in (0, 1)]
    greet(ring + [sib, side, up, down])

    def block(ref, comp, zz, yy, xx):
        return ref.at[comp, pl.ds(pl.multiple_of(((zz * 4 + yy) * 2 + xx) * rows, rows), rows)]

    def outgoing(hh, t, start):
        zt = 2 * core + hh
        slot = wrap(z - zt)
        i = hh * 2 + t
        pairs = (
            (kv_ref.at[t, hh], block(kvo_ref, t, z, y, xlo), zsend.at[i], zrecv.at[slot]),
            (q_ref.at[hh, t], qo_ref.at[z], qsend.at[i], qrecv.at[slot]),
        )
        here = jnp.logical_and(zt == z, core == t)

        for src, dst, ss, rs in pairs:
            @pl.when(here)
            def _():
                if start:
                    pltpu.make_async_copy(src, dst, rs).start()

            @pl.when(jnp.logical_not(here))
            def _():
                cp = remote(src, dst, ss, rs, device(xhi, xlo, y, zt, t))
                if start:
                    cp.start()
                else:
                    cp.wait_send()

    for hh in range(2):
        for t in range(2):
            outgoing(hh, t, True)

    sends = []

    def push(ref, ss, rs, peer):
        cp = remote(ref, ref, ss, rs, peer)
        cp.start()
        sends.append(cp)

    order = (0, 1, 3, 2)
    n = 0
    for i, d in enumerate(order):
        zz = wrap(z + d)
        ref = block(kvo_ref, core, zz, y, xlo)
        remote(kv_ref.at[0, 0], ref, zsend.at[0], zrecv.at[d], sib).wait_recv()
        push(ref, ypsend.at[i], yprecv.at[i], up)
        push(ref, ymsend.at[i], ymrecv.at[i], down)
        push(ref, xsend.at[i], xrecv.at[i], side)
        push(ref, bsend.at[n], brecv.at[n], sib)
        n += 1
    for i, d in enumerate(order):
        ref = block(kvo_ref, core, wrap(z + d), y, 1 - xlo)
        remote(ref, ref, xsend.at[i], xrecv.at[i], side).wait_recv()
        push(ref, ypsend.at[4 + i], yprecv.at[4 + i], up)
        push(ref, ymsend.at[4 + i], ymrecv.at[4 + i], down)
        push(ref, bsend.at[n], brecv.at[n], sib)
        n += 1
    for i in range(8):
        zz = wrap(z + order[i % 4])
        xx = xlo if i < 4 else 1 - xlo
        ref = block(kvo_ref, core, zz, wrap(y - 1), xx)
        remote(ref, ref, ypsend.at[i], yprecv.at[i], up).wait_recv()
        if i % 2 == 0:
            push(ref, fsend.at[i], frecv.at[i], up)
        push(ref, bsend.at[n], brecv.at[n], sib)
        n += 1
        ref = block(kvo_ref, core, zz, wrap(y + 1), xx)
        remote(ref, ref, ymsend.at[i], ymrecv.at[i], down).wait_recv()
        if i % 2 == 1:
            push(ref, fsend.at[i], frecv.at[i], down)
        push(ref, bsend.at[n], brecv.at[n], sib)
        n += 1
    for i in range(8):
        zz = wrap(z + order[i % 4])
        xx = xlo if i < 4 else 1 - xlo
        ref = block(kvo_ref, core, zz, wrap(y + 2), xx)
        remote(ref, ref, fsend.at[i], frecv.at[i], up).wait_recv()
        push(ref, bsend.at[n], brecv.at[n], sib)
        n += 1
    m = 0
    places = [(d, 0, 0) for d in order] + [(d, 0, 1) for d in order]
    for i in range(8):
        places += [(order[i % 4], 3, i // 4), (order[i % 4], 1, i // 4)]
    places += [(order[i % 4], 2, i // 4) for i in range(8)]
    for d, dy, other in places:
        xx = 1 - xlo if other else xlo
        ref = block(kvo_ref, 1 - core, wrap(z + d), wrap(y + dy), xx)
        remote(ref, ref, bsend.at[m], brecv.at[m], sib).wait_recv()
        m += 1
    for d in range(4):
        zz = wrap(z + d)
        remote(q_ref.at[0, 0], qo_ref.at[zz], qsend.at[0], qrecv.at[d], sib).wait_recv()
    for cp in sends:
        cp.wait_send()
    for hh in range(2):
        for t in range(2):
            outgoing(hh, t, False)


def attend_kernel(docs_ref, q_ref, k_ref, v_ref, o_ref, vt_ref):
    keys = k_ref.shape[0]
    m_rows = GROUP * QR
    tiles = q_ref.shape[0] // m_rows
    xhi, xlo, y, z, core = position()
    docs = docs_ref[...]
    b = [jnp.sum((docs < i).astype(jnp.int32)) for i in (1, 2, 3)]

    def start_of(p):
        return jnp.where(p >= b[2], b[2], jnp.where(p >= b[1], b[1], jnp.where(p >= b[0], b[0], 0)))

    tb = 512

    @pl.loop(0, keys // tb)
    def _(i):
        o = pl.multiple_of(i * tb, tb)
        vt_ref[:, pl.ds(o, tb)] = v_ref[pl.ds(o, tb), :].T

    c2 = (HD ** -0.5) * math.log2(math.e)
    per = tiles // 4
    plane = keys // 4
    block = plane // 8

    @pl.loop(0, tiles)
    def _(t):
        q0 = (
            lax.div(t, per) * plane + y * (2 * block) + xlo * block
            + (lax.rem(t, per) * 2 + core) * QR
        )
        q = q_ref[pl.ds(pl.multiple_of(t * m_rows, m_rows), m_rows), :]
        first, last = start_of(q0), start_of(q0 + QR - 1)
        t0 = first // KB
        t3 = (q0 + QR + KB - 1) // KB
        t1 = jnp.minimum((last + KB - 1) // KB, t3)
        t2 = jnp.maximum((q0 + 1) // KB, t1)
        qpos = q0 + lax.rem(lax.broadcasted_iota(jnp.int32, (1, m_rows), 1), QR)
        qst = start_of(qpos)

        def body(masked, i, carry):
            m, l, acc = carry
            o = pl.multiple_of(i * KB, KB)
            s = lax.dot_general(
                k_ref[pl.ds(o, KB), :], q, (((1,), (1,)), ((), ())), preferred_element_type=F32
            )
            if masked:
                kp = o + lax.broadcasted_iota(jnp.int32, (KB, m_rows), 0)
                s = jnp.where((kp <= qpos) & (kp >= qst), s, -1e30)
            mn = jnp.maximum(m, jnp.max(s, axis=0, keepdims=True))
            p = jnp.exp2((s - mn) * c2)
            a = jnp.exp2((m - mn) * c2)
            l = l * a + jnp.sum(p, axis=0, keepdims=True)
            acc = acc * a + jnp.dot(
                vt_ref[:, pl.ds(o, KB)], p.astype(BF16), preferred_element_type=F32
            )
            return mn, l, acc

        carry = (
            jnp.full((1, m_rows), -1e29, F32),
            jnp.zeros((1, m_rows), F32),
            jnp.zeros((HD, m_rows), F32),
        )
        carry = lax.fori_loop(t0, t1, functools.partial(body, True), carry)
        carry = lax.fori_loop(t1, t2, functools.partial(body, False), carry)
        m, l, acc = lax.fori_loop(t2, t3, functools.partial(body, True), carry)
        r = (acc / l).T.astype(BF16)
        ro = pl.multiple_of(t * QR, QR)
        for g in range(GROUP):
            o_ref[pl.ds(ro, QR), g * HD:(g + 1) * HD] = r[g * QR:(g + 1) * QR]


def output_kernel(
    att_ref, x_ref, w_hbm, o_ref,
    abuf, w, mine, theirs, part, recv_part, opp_part,
    wsem, asend, arecv, ssend, srecv, osend, orecv,
):
    xhi, xlo, y, z, core = position()
    sib, opp = device(xhi, xlo, y, z, 1 - core), device(1 - xhi, xlo, y, z, core)
    nj = att_ref.shape[1]
    width = x_ref.shape[1]
    owner = lax.div(z, 2)
    hz = lax.rem(z, 2)
    depth = w_hbm.shape[0]
    ncol = w_hbm.shape[1] // width
    loads = [
        pltpu.make_async_copy(
            w_hbm.at[:, pl.ds(pl.multiple_of(c * width, width), width)], w.at[i], wsem.at[i]
        )
        for i, c in enumerate(
            ((1 - xhi) * 2 + 1 - core, (1 - xhi) * 2 + core, xhi * 2 + 1 - core, xhi * 2 + core)
        )
    ]
    for load in loads:
        load.start()
    ring = [device(xhi, xlo, y, wrap(z + d), c) for d in (1, 2, 3) for c in (0, 1)]
    greet(ring + [sib, opp])

    def returning(d, j, start):
        zt = wrap(z + d)
        i = j * 4 + d
        src, dst = att_ref.at[zt, j], abuf.at[j, hz, core]
        slot = (j * 2 + hz) * 2 + core
        here = owner == core
        if d == 0:
            @pl.when(here)
            def _():
                if start:
                    pltpu.make_async_copy(src, dst, arecv.at[slot]).start()

            @pl.when(jnp.logical_not(here))
            def _():
                cp = remote(src, dst, asend.at[i], arecv.at[slot], sib)
                if start:
                    cp.start()
                else:
                    cp.wait_send()
        else:
            cp = remote(src, dst, asend.at[i], arecv.at[slot], device(xhi, xlo, y, zt, owner))
            if start:
                cp.start()
            else:
                cp.wait_send()

    for j in range(nj):
        for d in (1, 3, 2, 0):
            returning(d, j, True)
    waits = []
    opps = []
    for j in range(nj):
        for hh in range(2):
            for c in range(2):
                slot = (j * 2 + hh) * 2 + c
                remote(
                    att_ref.at[0, j], abuf.at[j, hh, c], asend.at[0], arecv.at[slot], sib
                ).wait_recv()

        def product(i):
            if j == 0:
                loads[i].wait()
            lhs = [
                jnp.concatenate([abuf[j, hh, 0], abuf[j, hh, 1]], axis=0) for hh in range(2)
            ]
            half = depth // 2
            return jnp.dot(lhs[0], w[i, :half], preferred_element_type=F32) + jnp.dot(
                lhs[1], w[i, half:], preferred_element_type=F32
            )

        for i in range(2):
            part[j, i] = product(2 * i).astype(BF16)
            cp = remote(part.at[j, i], recv_part.at[j, i], ssend.at[2 * j + i], srecv.at[2 * j + i], sib)
            cp.start()
            waits.append(cp)
            total = product(2 * i + 1)
            remote(
                part.at[j, i], recv_part.at[j, i], ssend.at[2 * j + i], srecv.at[2 * j + i], sib
            ).wait_recv()
            total = total + recv_part[j, i].astype(F32)
            if i == 0:
                theirs[j] = total.astype(BF16)
                cp = remote(theirs.at[j], opp_part.at[j], osend.at[j], orecv.at[j], opp)
                cp.start()
                opps.append(cp)
            else:
                mine[j] = total
    n = 2 * QR
    for j in range(nj):
        remote(theirs.at[j], opp_part.at[j], osend.at[j], orecv.at[j], opp).wait_recv()
        o_ref[j * n:(j + 1) * n, :] = (
            mine[j] + opp_part[j].astype(F32) + x_ref[j * n:(j + 1) * n, :].astype(F32)
        ).astype(BF16)
    for cp in waits + opps:
        cp.wait_send()
    for j in range(nj):
        for d in range(4):
            returning(d, j, False)


def vmem():
    return pl.BlockSpec(memory_space=pltpu.VMEM)


def hbm():
    return pl.BlockSpec(memory_space=pl.ANY)


def dma(n):
    return pltpu.SemaphoreType.DMA((n,))


def on_device(tables, tokens, doc_ids, norm_gain, w_query, w_key, w_value, w_out):
    rows, width = tokens.shape
    nch = 2
    ch = rows // nch
    keys = doc_ids.shape[0]
    blk = (rows // 2) * GROUP
    q, kv = pl.pallas_call(
        project_kernel,
        out_shape=(
            jax.ShapeDtypeStruct((2, 2, blk, HD), BF16),
            jax.ShapeDtypeStruct((2, 2, rows, HD), BF16),
        ),
        in_specs=[vmem()] * 6 + [hbm()] * 3,
        out_specs=(vmem(), vmem()),
        scratch_shapes=[
            pltpu.VMEM((nch, 4, ch, width), BF16),
            pltpu.VMEM((ch, 4 * width), BF16),
            pltpu.VMEM(w_query.shape, BF16),
            pltpu.VMEM(w_key.shape, BF16),
            pltpu.VMEM(w_value.shape, BF16),
            dma(3), dma(nch), dma(nch), dma(nch), dma(nch), dma(nch), dma(nch), dma(nch),
        ],
        compiler_params=pltpu.CompilerParams(
            collective_id=0, has_side_effects=True, vmem_limit_bytes=VMEM_LIMIT
        ),
        name="project",
    )(tokens, norm_gain.reshape(1, -1), *tables, w_query, w_key, w_value)
    q, kv = pl.pallas_call(
        exchange_kernel,
        out_shape=(
            jax.ShapeDtypeStruct((4, blk, HD), BF16),
            jax.ShapeDtypeStruct((2, keys, HD), BF16),
        ),
        in_specs=[hbm()] * 2,
        out_specs=(hbm(), hbm()),
        scratch_shapes=[
            dma(4), dma(4), dma(4), dma(4), dma(4), dma(4),
            dma(8), dma(8), dma(8), dma(8), dma(8), dma(8), dma(32), dma(32),
        ],
        compiler_params=pltpu.CompilerParams(collective_id=1, has_side_effects=True),
        name="exchange",
    )(q, kv)
    attended = pl.pallas_call(
        attend_kernel,
        out_shape=jax.ShapeDtypeStruct((4 * rows // 2, GROUP * HD), BF16),
        in_specs=[
            vmem(),
            vmem(),
            pl.BlockSpec((None, keys, HD), lambda i: (0, 0, 0)),
            pl.BlockSpec((None, keys, HD), lambda i: (1, 0, 0)),
        ],
        grid=(1,),
        out_specs=vmem(),
        scratch_shapes=[pltpu.VMEM((HD, keys), BF16)],
        compiler_params=pltpu.CompilerParams(vmem_limit_bytes=VMEM_LIMIT),
        name="attend",
    )(doc_ids.reshape(-1, 128), q.reshape(4 * blk, HD), kv, kv)
    nj = rows // (2 * QR)
    n = 2 * QR
    return pl.pallas_call(
        output_kernel,
        out_shape=jax.ShapeDtypeStruct((rows, width), BF16),
        in_specs=[hbm(), vmem(), hbm()],
        out_specs=vmem(),
        scratch_shapes=[
            pltpu.VMEM((nj, 2, 2, QR, GROUP * HD), BF16),
            pltpu.VMEM((4, w_out.shape[0], width), BF16),
            pltpu.VMEM((nj, n, width), F32),
            pltpu.VMEM((nj, n, width), BF16),
            pltpu.VMEM((nj, 2, n, width), BF16),
            pltpu.VMEM((nj, 2, n, width), BF16),
            pltpu.VMEM((nj, n, width), BF16),
            dma(4), dma(4 * nj), dma(4 * nj), dma(2 * nj), dma(2 * nj), dma(nj), dma(nj),
        ],
        compiler_params=pltpu.CompilerParams(
            collective_id=2, has_side_effects=True, vmem_limit_bytes=VMEM_LIMIT
        ),
        name="output",
    )(attended.reshape(4, nj, QR, GROUP * HD), tokens, w_out)


def solution(mesh):
    tables = rope_tables(384, mesh.shape["ctx"])

    def body(*args):
        return on_device(tuple(jnp.asarray(t) for t in tables), *args)

    in_specs = (
        P("ctx", "head"),
        P(),
        P(),
        P(None, "head"),
        P(None, "head"),
        P(None, "head"),
        P("head", None),
    )
    return jax.shard_map(
        body, mesh=mesh, in_specs=in_specs, out_specs=P("ctx", "head"), check_vma=False
    )
```

```python
import functools
import math

import jax
import jax.numpy as jnp
import numpy as np
from jax import lax
from jax.experimental import pallas as pl
from jax.experimental.pallas import tpu as pltpu
from jax.sharding import PartitionSpec as P

MESH = pl.DeviceIdType.MESH
BF16 = jnp.bfloat16
F32 = jnp.float32
HD = 128
GROUP = 4
THETA = 500000.0
QR = 96
KB = 1024
LATE = (3,)
PR = 48
VMEM_LIMIT = 60 * 2**20


def position():
    c, h = lax.axis_index("ctx"), lax.axis_index("head")
    return lax.div(h, 2), lax.rem(c, 2), lax.rem(lax.div(c, 2), 4), lax.div(c, 8), lax.rem(h, 2)


def device(xhi, xlo, y, z, core):
    return {"ctx": (z * 4 + y) * 2 + xlo, "head": xhi * 2 + core}


def wrap(v):
    return lax.rem(v + 4, 4)


def greet(peers):
    barrier = pltpu.get_barrier_semaphore()
    for peer in peers:
        pl.semaphore_signal(barrier, inc=1, device_id=peer, device_id_type=MESH)
    pl.semaphore_wait(barrier, len(peers))


def remote(src, dst, send, recv, peer):
    return pltpu.make_async_remote_copy(
        src_ref=src, dst_ref=dst, send_sem=send, recv_sem=recv, device_id=peer, device_id_type=MESH
    )


def rope_tables(rows, blocks):
    inverse = THETA ** (-np.arange(HD // 2, dtype=np.float64) / (HD // 2))
    near = np.arange(rows, dtype=np.float64)[:, None] * inverse[None, :]
    far = (np.arange(blocks, dtype=np.float64) * rows)[:, None] * inverse[None, :]

    def pair(a):
        return (
            np.concatenate([np.cos(a), np.cos(a)], 1).astype(np.float32),
            np.concatenate([np.sin(a), np.sin(a)], 1).astype(np.float32),
        )

    return pair(near) + pair(far)


def gather_kernel(
    x_ref, gain_ref, cn_ref, sn_ref, cf_ref, sf_ref, wq_hbm, wk_hbm, wv_hbm,
    qo_ref, kvo_ref,
    xbuf, nbuf, wq, wk, wv, qbuf, kvbuf,
    wsem, lsem, ssend, srecv, osend, orecv, tsend, trecv,
    zsend, zrecv, qsend, qrecv, xsend, xrecv, ypsend, yprecv, ymsend, ymrecv, fsend, frecv, bsend, brecv,
):
    xhi, xlo, y, z, core = position()
    head = xhi * 2 + core
    rows, width = x_ref.shape
    nch = xbuf.shape[0]
    ch = rows // nch
    sib, opp = device(xhi, xlo, y, z, 1 - core), device(1 - xhi, xlo, y, z, core)
    side = device(xhi, 1 - xlo, y, z, core)
    up, down = device(xhi, xlo, wrap(y + 1), z, core), device(xhi, xlo, wrap(y - 1), z, core)
    ring = [device(xhi, xlo, y, wrap(z + d), c) for d in (1, 2, 3) for c in (0, 1)]
    hs, ho, hf = xhi * 2 + 1 - core, (1 - xhi) * 2 + core, (1 - xhi) * 2 + 1 - core
    loads = [
        pltpu.make_async_copy(a, b, wsem.at[i])
        for i, (a, b) in enumerate(((wk_hbm, wk), (wv_hbm, wv), (wq_hbm, wq)))
    ]
    for load in loads:
        load.start()
    greet(ring + [sib, opp, side, up, down])
    sends = []

    def rows_of(k):
        return x_ref.at[pl.ds(k * ch, ch)]

    owns = []
    for k in range(nch):
        cp = remote(rows_of(k), xbuf.at[k, head], osend.at[k], orecv.at[k], opp)
        cp.start()
        sends.append(cp)
    for k in range(nch):
        cp = remote(rows_of(k), xbuf.at[k, head], ssend.at[k], srecv.at[k], sib)
        cp.start()
        sends.append(cp)
        owns.append(pltpu.make_async_copy(rows_of(k), xbuf.at[k, head], lsem.at[k]))
        owns[k].start()
    cn, sn = cn_ref[...], sn_ref[...]
    ctx = lax.axis_index("ctx")
    cf, sf = cf_ref[pl.ds(ctx, 1), :], sf_ref[pl.ds(ctx, 1), :]
    cos = cn * cf - sn * sf
    sin = sn * cf + cn * sf
    lane = lax.broadcasted_iota(jnp.int32, (rows, HD), 1)
    sin = jnp.where(lane < HD // 2, -sin, sin)

    def rope(v, k):
        lo = k * ch
        return v * cos[lo:lo + ch] + pltpu.roll(v, HD // 2, 1) * sin[lo:lo + ch]

    def norm(k):
        remote(rows_of(k), xbuf.at[k, ho], osend.at[k], orecv.at[k], opp).wait_recv()
        cp = remote(xbuf.at[k, ho], xbuf.at[k, ho], tsend.at[k], trecv.at[k], sib)
        cp.start()
        sends.append(cp)
        owns[k].wait()
        remote(rows_of(k), xbuf.at[k, hs], ssend.at[k], srecv.at[k], sib).wait_recv()
        remote(xbuf.at[k, ho], xbuf.at[k, hf], tsend.at[k], trecv.at[k], sib).wait_recv()
        total = jnp.zeros((ch, 1), F32)
        for j in range(4):
            v = xbuf[k, j].astype(F32)
            total = total + jnp.sum(v * v, axis=1, keepdims=True)
        scale = lax.rsqrt(total / (4.0 * width) + 1e-05)
        for j in range(4):
            v = xbuf[k, j].astype(F32)
            nbuf[:, j * width:(j + 1) * width] = (
                v * scale * gain_ref[:, j * width:(j + 1) * width]
            ).astype(BF16)

    def project_kv(k):
        if k == 0:
            loads[0].wait()
            loads[1].wait()
        kk = jnp.dot(nbuf[...], wk[...], preferred_element_type=F32)
        vv = jnp.dot(nbuf[...], wv[...], preferred_element_type=F32)
        for hh in range(2):
            kvbuf[0, hh, k] = rope(kk[:, hh * HD:(hh + 1) * HD], k).astype(BF16)
            kvbuf[1, hh, k] = vv[:, hh * HD:(hh + 1) * HD].astype(BF16)

    def project_q(k, pairs):
        if k == 0 and pairs == 0:
            loads[2].wait()
        qq = jnp.dot(
            nbuf[...], wq[:, pairs * 256:(pairs + 1) * 256], preferred_element_type=F32
        )
        for u in range(2):
            g = (pairs % 2) * 2 + u
            out = rope(qq[:, u * HD:(u + 1) * HD], k).astype(BF16)
            for b in range(ch // QR):
                at = (b // 2) * GROUP * QR + g * QR
                qbuf[pairs // 2, b % 2, k, at:at + QR, :] = out[b * QR:(b + 1) * QR]

    def block(comp, d, dy, other, k):
        zz, yy = wrap(z + d), wrap(y + dy)
        xx = 1 - xlo if other else xlo
        at = ((zz * 4 + yy) * 2 + xx) * rows + k * ch
        return kvo_ref.at[comp, pl.ds(pl.multiple_of(at, ch), ch)]

    def outgoing(k, keys, start, only=None):
        for hh in range(2) if only is None else (only,):
            zt = 2 * core + hh
            slot = wrap(z - zt)
            for t in range(2):
                i = hh * 2 + t
                if keys:
                    src, dst, ss, rs = (
                        kvbuf.at[t, hh, k], block(t, 0, 0, 0, k), zsend.at[k, i], zrecv.at[k, slot]
                    )
                else:
                    src, dst, ss, rs = (
                        qbuf.at[hh, t, k], qo_ref.at[z, k], qsend.at[k, i], qrecv.at[k, slot]
                    )
                here = jnp.logical_and(zt == z, core == t)
                if start:
                    @pl.when(here)
                    def _():
                        pltpu.make_async_copy(src, dst, rs).start()

                @pl.when(jnp.logical_not(here))
                def _():
                    cp = remote(src, dst, ss, rs, device(xhi, xlo, y, zt, t))
                    if start:
                        cp.start()
                    else:
                        cp.wait_send()

    def push(ref, ss, rs, peer):
        cp = remote(ref, ref, ss, rs, peer)
        cp.start()
        sends.append(cp)

    order = (0, 1, 3, 2)
    passed = []

    def share(k, d, dy, other):
        n = len(passed)
        passed.append((k, d, dy, other))
        push(block(core, d, dy, other, k), bsend.at[n], brecv.at[n], sib)

    def from_z(k):
        for i, d in enumerate(order):
            ref = block(core, d, 0, 0, k)
            remote(kvbuf.at[0, 0, k], ref, zsend.at[k, 0], zrecv.at[k, d], sib).wait_recv()
            push(ref, xsend.at[k, i], xrecv.at[k, i], side)
            push(ref, ypsend.at[k, i], yprecv.at[k, i], up)
            push(ref, ymsend.at[k, i], ymrecv.at[k, i], down)
            share(k, d, 0, 0)

    def from_x(k):
        for i, d in enumerate(order):
            ref = block(core, d, 0, 1, k)
            remote(ref, ref, xsend.at[k, i], xrecv.at[k, i], side).wait_recv()
            if i not in LATE:
                push(ref, ypsend.at[k, 4 + i], yprecv.at[k, 4 + i], up)
                push(ref, ymsend.at[k, 4 + i], ymrecv.at[k, 4 + i], down)
            share(k, d, 0, 1)

    def late_slot(i, dy):
        return 4 + LATE.index(i) * 3 + dy - 1

    def from_y(k):
        for i in range(8):
            d, other = order[i % 4], i // 4
            if other and i % 4 in LATE:
                continue
            ref = block(core, d, 3, other, k)
            remote(ref, ref, ypsend.at[k, i], yprecv.at[k, i], up).wait_recv()
            if i % 2 == 0:
                push(ref, fsend.at[k, i], frecv.at[k, i], up)
            if i in LATE:
                push(ref, xsend.at[k, late_slot(i, 3)], xrecv.at[k, late_slot(i, 3)], side)
            share(k, d, 3, other)
            ref = block(core, d, 1, other, k)
            remote(ref, ref, ymsend.at[k, i], ymrecv.at[k, i], down).wait_recv()
            if i % 2 == 1:
                push(ref, fsend.at[k, i], frecv.at[k, i], down)
            if i in LATE:
                push(ref, xsend.at[k, late_slot(i, 1)], xrecv.at[k, late_slot(i, 1)], side)
            share(k, d, 1, other)

    def from_far(k):
        for i in range(8):
            if i >= 4 and i % 4 in LATE:
                continue
            ref = block(core, order[i % 4], 2, i // 4, k)
            remote(ref, ref, fsend.at[k, i], frecv.at[k, i], up).wait_recv()
            if i in LATE:
                push(ref, xsend.at[k, late_slot(i, 2)], xrecv.at[k, late_slot(i, 2)], side)
            share(k, order[i % 4], 2, i // 4)

    def from_late(k):
        for i in LATE:
            for dy in (3, 1, 2):
                ref = block(core, order[i], dy, 1, k)
                n = late_slot(i, dy)
                remote(ref, ref, xsend.at[k, n], xrecv.at[k, n], side).wait_recv()
                share(k, order[i], dy, 1)

    norm(0)
    project_kv(0)
    project_q(0, 0)
    outgoing(0, True, True)
    project_q(0, 1)
    project_q(0, 2)
    outgoing(0, False, True, 0)
    project_q(0, 3)
    from_z(0)
    outgoing(0, False, True, 1)
    norm(1)
    project_kv(1)
    from_x(0)
    outgoing(1, True, True)
    project_q(1, 0)
    project_q(1, 1)
    from_y(0)
    from_z(1)
    outgoing(1, False, True, 0)
    project_q(1, 2)
    project_q(1, 3)
    from_x(1)
    outgoing(1, False, True, 1)
    from_far(0)
    from_y(1)
    from_late(0)
    from_far(1)
    from_late(1)
    for m, (k, d, dy, other) in enumerate(passed):
        ref = block(1 - core, d, dy, other, k)
        remote(ref, ref, bsend.at[m], brecv.at[m], sib).wait_recv()
    for k in range(nch):
        for d in range(4):
            remote(
                qbuf.at[0, 0, k], qo_ref.at[wrap(z + d), k], qsend.at[k, 0], qrecv.at[k, d], sib
            ).wait_recv()
    for cp in sends:
        cp.wait_send()
    for k in range(nch):
        outgoing(k, True, False)
        outgoing(k, False, False)


def attend_kernel(docs_ref, q_ref, k_ref, v_ref, o_ref, vt_ref, sa_ref, sb_ref):
    keys = k_ref.shape[0]
    m_rows = GROUP * QR
    tiles = q_ref.shape[0] // m_rows
    xhi, xlo, y, z, core = position()
    docs = docs_ref[...]
    b = [jnp.sum((docs < i).astype(jnp.int32)) for i in (1, 2, 3)]

    def start_of(p):
        return jnp.where(p >= b[2], b[2], jnp.where(p >= b[1], b[1], jnp.where(p >= b[0], b[0], 0)))

    tb = 512

    @pl.loop(0, keys // tb)
    def _(i):
        o = pl.multiple_of(i * tb, tb)
        vt_ref[:, pl.ds(o, tb)] = v_ref[pl.ds(o, tb), :].T

    c2 = (HD ** -0.5) * math.log2(math.e)
    per = tiles // 4
    plane = keys // 4
    block = plane // 8
    half = KB // 2

    @pl.loop(0, tiles)
    def _(t):
        q0 = (
            lax.div(t, per) * plane + y * (2 * block) + xlo * block
            + (lax.rem(t, per) * 2 + core) * QR
        )
        q = q_ref[pl.ds(pl.multiple_of(t * m_rows, m_rows), m_rows), :]
        first, last = start_of(q0), start_of(q0 + QR - 1)
        t0 = first // KB
        t3 = (q0 + QR + KB - 1) // KB
        t1 = jnp.minimum((last + KB - 1) // KB, t3)
        t2 = jnp.maximum((q0 + 1) // KB, t1)
        qpos = q0 + lax.rem(lax.broadcasted_iota(jnp.int32, (1, m_rows), 1), QR)
        qst = start_of(qpos)

        def score(o):
            return lax.dot_general(
                k_ref[pl.ds(pl.multiple_of(o, half), half), :],
                q, (((1,), (1,)), ((), ())), preferred_element_type=F32,
            )

        def absorb(masked, s_ref, o, carry):
            m, l, acc = carry
            s = s_ref[...]
            if masked:
                kp = o + lax.broadcasted_iota(jnp.int32, (half, m_rows), 0)
                s = jnp.where((kp <= qpos) & (kp >= qst), s, -1e30)
            mn = jnp.maximum(m, jnp.max(s, axis=0, keepdims=True))
            p = jnp.exp2((s - mn) * c2)
            a = jnp.exp2((m - mn) * c2)
            l = l * a + jnp.sum(p, axis=0, keepdims=True)
            acc = acc * a + jnp.dot(
                vt_ref[:, pl.ds(pl.multiple_of(o, half), half)],
                p.astype(BF16), preferred_element_type=F32,
            )
            return mn, l, acc

        def body(masked, i, carry):
            o = i * KB
            sb_ref[...] = score(o + half)
            carry = absorb(masked, sa_ref, o, carry)
            sa_ref[...] = score(jnp.minimum(o + KB, keys - half))
            return absorb(masked, sb_ref, o + half, carry)

        sa_ref[...] = score(t0 * KB)
        carry = (
            jnp.full((1, m_rows), -1e29, F32),
            jnp.zeros((1, m_rows), F32),
            jnp.zeros((HD, m_rows), F32),
        )
        carry = lax.fori_loop(t0, t1, functools.partial(body, True), carry)
        carry = lax.fori_loop(t1, t2, functools.partial(body, False), carry)
        m, l, acc = lax.fori_loop(t2, t3, functools.partial(body, True), carry)
        r = (acc / l).T.astype(BF16)
        ro = pl.multiple_of(t * QR, QR)
        for g in range(GROUP):
            o_ref[pl.ds(ro, QR), g * HD:(g + 1) * HD] = r[g * QR:(g + 1) * QR]


def output_kernel(
    att_ref, x_ref, w_hbm, o_ref,
    abuf, w, mine, theirs, part, recv_part, opp_part,
    wsem, asend, arecv, ssend, srecv, osend, orecv,
):
    xhi, xlo, y, z, core = position()
    sib, opp = device(xhi, xlo, y, z, 1 - core), device(1 - xhi, xlo, y, z, core)
    nj = att_ref.shape[1]
    parts = QR // PR
    width = x_ref.shape[1]
    owner = lax.div(z, 2)
    hz = lax.rem(z, 2)
    depth = w_hbm.shape[0]
    ncol = w_hbm.shape[1] // width
    loads = [
        pltpu.make_async_copy(
            w_hbm.at[:, pl.ds(pl.multiple_of(c * width, width), width)], w.at[i], wsem.at[i]
        )
        for i, c in enumerate(
            ((1 - xhi) * 2 + 1 - core, (1 - xhi) * 2 + core, xhi * 2 + 1 - core, xhi * 2 + core)
        )
    ]
    for load in loads:
        load.start()
    ring = [device(xhi, xlo, y, wrap(z + d), c) for d in (1, 2, 3) for c in (0, 1)]
    greet(ring + [sib, opp])

    def returning(d, j, start):
        zt = wrap(z + d)
        i = j * 4 + d
        src, dst = att_ref.at[zt, j], abuf.at[j, hz, core]
        slot = (j * 2 + hz) * 2 + core
        here = owner == core
        if d == 0:
            @pl.when(here)
            def _():
                if start:
                    pltpu.make_async_copy(src, dst, arecv.at[slot]).start()

            @pl.when(jnp.logical_not(here))
            def _():
                cp = remote(src, dst, asend.at[i], arecv.at[slot], sib)
                if start:
                    cp.start()
                else:
                    cp.wait_send()
        else:
            cp = remote(src, dst, asend.at[i], arecv.at[slot], device(xhi, xlo, y, zt, owner))
            if start:
                cp.start()
            else:
                cp.wait_send()

    for j in range(nj):
        for d in (1, 3, 2, 0):
            returning(d, j, True)
    waits = []
    opps = []
    for j in range(nj):
        for hh in range(2):
            for c in range(2):
                slot = (j * 2 + hh) * 2 + c
                remote(
                    att_ref.at[0, j], abuf.at[j, hh, c], asend.at[0], arecv.at[slot], sib
                ).wait_recv()

        def product(i):
            if j == 0:
                loads[i].wait()
            lhs = [
                jnp.concatenate([abuf[j, hh, 0], abuf[j, hh, 1]], axis=0) for hh in range(2)
            ]
            half = depth // 2
            return jnp.dot(lhs[0], w[i, :half], preferred_element_type=F32) + jnp.dot(
                lhs[1], w[i, half:], preferred_element_type=F32
            )

        for i in range(2):
            part[j, i] = product(2 * i).astype(BF16)
            cp = remote(part.at[j, i], recv_part.at[j, i], ssend.at[2 * j + i], srecv.at[2 * j + i], sib)
            cp.start()
            waits.append(cp)
            total = product(2 * i + 1)
            remote(
                part.at[j, i], recv_part.at[j, i], ssend.at[2 * j + i], srecv.at[2 * j + i], sib
            ).wait_recv()
            total = total + recv_part[j, i].astype(F32)
            if i == 0:
                theirs[j] = total.astype(BF16)
                cp = remote(theirs.at[j], opp_part.at[j], osend.at[j], orecv.at[j], opp)
                cp.start()
                opps.append(cp)
            else:
                mine[j] = total
    for j in range(nj):
        remote(theirs.at[j], opp_part.at[j], osend.at[j], orecv.at[j], opp).wait_recv()
        for c in range(2):
            at = (j // parts * 2 + c) * QR + j % parts * PR
            lo = c * PR
            o_ref[at:at + PR, :] = (
                mine[j, lo:lo + PR] + opp_part[j, lo:lo + PR].astype(F32)
                + x_ref[at:at + PR, :].astype(F32)
            ).astype(BF16)
    for cp in waits + opps:
        cp.wait_send()
    for j in range(nj):
        for d in range(4):
            returning(d, j, False)


def vmem():
    return pl.BlockSpec(memory_space=pltpu.VMEM)


def hbm():
    return pl.BlockSpec(memory_space=pl.ANY)


def dma(*n):
    return pltpu.SemaphoreType.DMA(n)


def on_device(tables, tokens, doc_ids, norm_gain, w_query, w_key, w_value, w_out):
    rows, width = tokens.shape
    nch = 2
    ch = rows // nch
    keys = doc_ids.shape[0]
    blk = (rows // 2) * GROUP
    q, kv = pl.pallas_call(
        gather_kernel,
        out_shape=(
            jax.ShapeDtypeStruct((4, nch, blk // nch, HD), BF16),
            jax.ShapeDtypeStruct((2, keys, HD), BF16),
        ),
        in_specs=[vmem()] * 6 + [hbm()] * 3,
        out_specs=(hbm(), hbm()),
        scratch_shapes=[
            pltpu.VMEM((nch, 4, ch, width), BF16),
            pltpu.VMEM((ch, 4 * width), BF16),
            pltpu.VMEM(w_query.shape, BF16),
            pltpu.VMEM(w_key.shape, BF16),
            pltpu.VMEM(w_value.shape, BF16),
            pltpu.VMEM((2, 2, nch, blk // nch, HD), BF16),
            pltpu.VMEM((2, 2, nch, ch, HD), BF16),
            dma(3), *[dma(nch)] * 7,
            *[dma(nch, 4)] * 4, *[dma(nch, 4 + 3 * len(LATE))] * 2, *[dma(nch, 8)] * 6, *[dma(32 * nch)] * 2,
        ],
        compiler_params=pltpu.CompilerParams(
            collective_id=0, has_side_effects=True, vmem_limit_bytes=VMEM_LIMIT
        ),
        name="gather",
    )(tokens, norm_gain.reshape(1, -1), *tables, w_query, w_key, w_value)
    attended = pl.pallas_call(
        attend_kernel,
        out_shape=jax.ShapeDtypeStruct((4 * rows // 2, GROUP * HD), BF16),
        in_specs=[
            vmem(),
            vmem(),
            pl.BlockSpec((None, keys, HD), lambda i: (0, 0, 0)),
            pl.BlockSpec((None, keys, HD), lambda i: (1, 0, 0)),
        ],
        grid=(1,),
        out_specs=vmem(),
        scratch_shapes=[
            pltpu.VMEM((HD, keys), BF16),
            pltpu.VMEM((KB // 2, GROUP * QR), F32),
            pltpu.VMEM((KB // 2, GROUP * QR), F32),
        ],
        compiler_params=pltpu.CompilerParams(vmem_limit_bytes=VMEM_LIMIT),
        name="attend",
    )(doc_ids.reshape(-1, 128), q.reshape(4 * blk, HD), kv, kv)
    nj = rows // (2 * PR)
    n = 2 * PR
    return pl.pallas_call(
        output_kernel,
        out_shape=jax.ShapeDtypeStruct((rows, width), BF16),
        in_specs=[hbm(), vmem(), hbm()],
        out_specs=vmem(),
        scratch_shapes=[
            pltpu.VMEM((nj, 2, 2, PR, GROUP * HD), BF16),
            pltpu.VMEM((4, w_out.shape[0], width), BF16),
            pltpu.VMEM((nj, n, width), F32),
            pltpu.VMEM((nj, n, width), BF16),
            pltpu.VMEM((nj, 2, n, width), BF16),
            pltpu.VMEM((nj, 2, n, width), BF16),
            pltpu.VMEM((nj, n, width), BF16),
            dma(4), dma(4 * nj), dma(4 * nj), dma(2 * nj), dma(2 * nj), dma(nj), dma(nj),
        ],
        compiler_params=pltpu.CompilerParams(
            collective_id=1, has_side_effects=True, vmem_limit_bytes=VMEM_LIMIT
        ),
        name="output",
    )(attended.reshape(4, nj, PR, GROUP * HD), tokens, w_out)


def solution(mesh):
    tables = rope_tables(384, mesh.shape["ctx"])

    def body(*args):
        return on_device(tuple(jnp.asarray(t) for t in tables), *args)

    in_specs = (
        P("ctx", "head"),
        P(),
        P(),
        P(None, "head"),
        P(None, "head"),
        P(None, "head"),
        P("head", None),
    )
    return jax.shard_map(
        body, mesh=mesh, in_specs=in_specs, out_specs=P("ctx", "head"), check_vma=False
    )
```
